32 devices in a mesh: ctx: 8 (over z, y), head: 4 (over x, core).
Axes of the slice: x: 2, y: 2, z: 4, core: 2. Of those that a mesh axis runs over, the one named last changes fastest.
Arguments:
- activations: bfloat16 [8192, 2048], P(('ctx', 'head')), may hold values from -6 to 6
- w_query: bfloat16 [2048, 1024], P('ctx', 'head'), may hold values from -0.125 to 0.125
- w_key: bfloat16 [2048, 1024], P('ctx', 'head'), may hold values from -0.125 to 0.125
- w_value: bfloat16 [2048, 2048], P('ctx', 'head'), may hold values from -0.125 to 0.125
- w_zgate: bfloat16 [2048, 2048], P('ctx', 'head'), may hold values from -0.125 to 0.125
- conv_query: bfloat16 [4, 1024], P(None, 'head'), may hold values from -3 to 3
- conv_key: bfloat16 [4, 1024], P(None, 'head'), may hold values from -3 to 3
- conv_value: bfloat16 [4, 2048], P(None, 'head'), may hold values from -3 to 3
- gate_code: int32 [8192, 16], P('ctx', 'head'), may hold values from 0 to 726816
- beta_code: int32 [8192, 16], P('ctx', 'head'), may hold values from 0 to 65536
- norm_gain: float32 [128], replicated, may hold values from 0.1 to 1.9
- w_out: bfloat16 [2048, 2048], P('head', 'ctx'), may hold values from -0.125 to 0.125
Outputs:
- layer_out: bfloat16 [8192, 2048], P(('ctx', 'head'))
The draws below stay inside these ranges and needn't reach their ends.
All inputs are finite; a program needn't handle non-finite values.
Results may differ from the reference program's by a relative error of at most 0.012.
Values may be sent and summed in bfloat16 or wider, within the bound.
A program may use at most 192 MiB of HBM per device.

```python
import jax
import jax.numpy as jnp
from jax import lax

D = 2048
HK = 8
SHARD_OUTPUT_HEAD = 16
DK = 128
DV = 128
KW = 4
SPAN = 64
SEQUENCE_LENGTH = 8192


def head_speeds(key):
    return jax.random.randint(jax.random.fold_in(key, 11), (SHARD_OUTPUT_HEAD,), 0, 2)


def draw_gate_code(key, part):
    speeds = head_speeds(key)
    slow_code = jax.random.randint(jax.random.fold_in(key, 21), (SEQUENCE_LENGTH, SHARD_OUTPUT_HEAD), 0, 1048576 // SEQUENCE_LENGTH + 1)
    fast_code = jax.random.randint(jax.random.fold_in(key, 22), (SEQUENCE_LENGTH, SHARD_OUTPUT_HEAD), 1048576 // 50, 1048576 // 25 + 1)
    picked_group = jax.random.randint(jax.random.fold_in(key, 23), (SEQUENCE_LENGTH, SHARD_OUTPUT_HEAD), 0, SEQUENCE_LENGTH) < 2
    sampled_group_name = jax.random.randint(jax.random.fold_in(key, 24), (SEQUENCE_LENGTH, SHARD_OUTPUT_HEAD), 233017, 726817)
    picked_variant = jnp.where(speeds[None, :] == 1, fast_code, slow_code)
    return jnp.where(picked_group, sampled_group_name, picked_variant).astype(jnp.int32)


def draw_beta_code(key, part):
    speeds = head_speeds(key)
    slow_code = jax.random.randint(jax.random.fold_in(key, 31), (SEQUENCE_LENGTH, SHARD_OUTPUT_HEAD), 0, 65536 * DK // SEQUENCE_LENGTH + 1)
    fast_code = jax.random.randint(jax.random.fold_in(key, 32), (SEQUENCE_LENGTH, SHARD_OUTPUT_HEAD), 16384, 65537)
    return jnp.where(speeds[None, :] == 1, fast_code, slow_code).astype(jnp.int32)


def block_scale(stream_key, shape, pieces, smallest, top_value):
    gain, own = 1.0, jax.random.fold_in(stream_key, 6)
    for dim, blocks in pieces:
        draws = jnp.exp(jax.random.uniform(jax.random.fold_in(own, dim), (blocks,), jnp.float32, smallest / len(pieces), top_value / len(pieces)))
        gain = gain * jnp.repeat(draws, shape[dim] // blocks).reshape([-1 if axis == dim else 1 for axis in range(len(shape))])
    return gain


def bell_draw(rng, dims, scale, reach, split=(), kind=jnp.bfloat16):
    drawn = jax.random.normal(rng, dims, jnp.float32) * scale
    if len(split) > 0:
        drawn = block_scale(rng, dims, split, -0.22, 0.18) * drawn
    return jnp.clip(drawn, min=-reach, max=reach).astype(kind)


def setup_inputs(seed: int = 0) -> dict:
    arg_keys = jax.random.split(jax.random.key(seed), 13)
    return {
        "activations": bell_draw(arg_keys[0], (SEQUENCE_LENGTH, D), 1.0, 6.0, ((0, 32),)),
        "w_query": bell_draw(arg_keys[1], (D, HK * DK), D ** -0.5, 0.125, ((0, 8), (1, 4))),
        "w_key": bell_draw(arg_keys[2], (D, HK * DK), D ** -0.5, 0.125, ((0, 8), (1, 4))),
        "w_value": bell_draw(arg_keys[3], (D, SHARD_OUTPUT_HEAD * DV), D ** -0.5, 0.125, ((0, 8), (1, 4))),
        "w_zgate": bell_draw(arg_keys[4], (D, SHARD_OUTPUT_HEAD * DV), D ** -0.5, 0.125, ((0, 8), (1, 4))),
        "conv_query": bell_draw(arg_keys[5], (KW, HK * DK), KW ** -0.5, 3.0, ((1, 4),)),
        "conv_key": bell_draw(arg_keys[6], (KW, HK * DK), KW ** -0.5, 3.0, ((1, 4),)),
        "conv_value": bell_draw(arg_keys[7], (KW, SHARD_OUTPUT_HEAD * DV), KW ** -0.5, 3.0, ((1, 4),)),
        "gate_code": draw_gate_code(jax.random.fold_in(arg_keys[12], 71), 0),
        "beta_code": draw_beta_code(jax.random.fold_in(arg_keys[12], 71), 0),
        "norm_gain": jnp.clip(1.0 + 0.18 * jax.random.normal(arg_keys[10], (DV,), jnp.float32), 0.1, 1.9),
        "w_out": bell_draw(arg_keys[11], (SHARD_OUTPUT_HEAD * DV, D), (SHARD_OUTPUT_HEAD * DV) ** -0.5, 0.125, ((0, 4), (1, 8))),
    }


def contract(form, left, right):
    return jnp.einsum(form, left, right, precision=lax.Precision.HIGHEST)

def causal_conv(edge_rows, raw_rows, weights):
    tap_count = weights.shape[0]
    joined = jnp.concatenate([edge_rows, raw_rows], 0).astype(jnp.float32)
    length = raw_rows.shape[0]
    summed = jnp.zeros((length, raw_rows.shape[1]), jnp.float32)
    for offset in range(tap_count):
        summed = summed + joined[offset:offset + length] * weights[offset].astype(jnp.float32)
    return jax.nn.silu(summed).astype(jnp.bfloat16)

def span_terms(query_rows, key_rows, value_rows, log_gate, beta_rows):
    cumulated = jnp.cumsum(log_gate, axis=-1)
    length = log_gate.shape[-1]
    key_width = key_rows.shape[-1]
    positions = jnp.arange(length)
    strict_mask = positions[:, None] > positions[None, :]
    incl_mask = positions[:, None] >= positions[None, :]
    differences = cumulated[..., :, None] - cumulated[..., None, :]
    decay_strict = jnp.where(strict_mask, jnp.exp(jnp.where(strict_mask, differences, 0.0)), 0.0)
    decay_incl = jnp.where(incl_mask, jnp.exp(jnp.where(incl_mask, differences, 0.0)), 0.0)
    key_gram = contract('...id,...jd->...ij', key_rows, key_rows)
    mixing = beta_rows[..., :, None] * key_gram * decay_strict
    identity_block = jnp.eye(length, dtype=jnp.float32)
    right_hand = jnp.concatenate([key_rows * (beta_rows * jnp.exp(cumulated))[..., None], value_rows * beta_rows[..., None]], -1)
    solved = jax.scipy.linalg.solve_triangular(identity_block + mixing, right_hand, lower=True, unit_diagonal=True)
    w_block = solved[..., :key_width]
    u_block = solved[..., key_width:]
    tail_decay = jnp.exp(cumulated[..., -1:] - cumulated)
    key_decayed = key_rows * tail_decay[..., None]
    eye_key = jnp.eye(key_width, dtype=jnp.float32)
    transition = jnp.exp(cumulated[..., -1])[..., None, None] * eye_key - contract('...cd,...ce->...de', key_decayed, w_block)
    written = contract('...cd,...ce->...de', key_decayed, u_block)
    scores = contract('...id,...jd->...ij', query_rows, key_rows) * decay_incl
    query_eff = query_rows * jnp.exp(cumulated)[..., None] - contract('...ij,...jd->...id', scores, w_block)
    local_out = contract('...ij,...jd->...id', scores, u_block)
    return (query_eff, local_out, transition, written)

def reference(activations, w_query, w_key, w_value, w_zgate, conv_query, conv_key, conv_value, gate_code, beta_code, norm_gain, w_out):
    query_proj = jnp.dot(activations.astype(jnp.float32), w_query.astype(jnp.float32), preferred_element_type=jnp.float32).astype(jnp.bfloat16)
    key_proj = jnp.dot(activations.astype(jnp.float32), w_key.astype(jnp.float32), preferred_element_type=jnp.float32).astype(jnp.bfloat16)
    value_proj = jnp.dot(activations.astype(jnp.float32), w_value.astype(jnp.float32), preferred_element_type=jnp.float32).astype(jnp.bfloat16)
    zgate_proj = jnp.dot(activations.astype(jnp.float32), w_zgate.astype(jnp.float32), preferred_element_type=jnp.float32).astype(jnp.bfloat16)
    query_conv = causal_conv(jnp.zeros((KW - 1, query_proj.shape[1]), jnp.bfloat16), query_proj, conv_query)
    key_conv = causal_conv(jnp.zeros((KW - 1, key_proj.shape[1]), jnp.bfloat16), key_proj, conv_key)
    convolved_value = causal_conv(jnp.zeros((KW - 1, value_proj.shape[1]), jnp.bfloat16), value_proj, conv_value)
    group_size = SHARD_OUTPUT_HEAD // HK
    blocks = SEQUENCE_LENGTH // SPAN

    def one_head(head_index):
        key_head = (head_index // group_size).astype(jnp.int32)
        query_rows = lax.dynamic_slice_in_dim(query_conv, key_head * DK, DK, 1).astype(jnp.float32)
        key_raw = lax.dynamic_slice_in_dim(key_conv, key_head * DK, DK, 1).astype(jnp.float32)
        key_rows = key_raw / jnp.sqrt(lax.optimization_barrier(jnp.sum(key_raw * key_raw, -1, keepdims=True)) + 1e-06)
        value_rows = lax.dynamic_slice_in_dim(convolved_value, head_index * DV, DV, 1).astype(jnp.float32)
        zgate_rows = lax.dynamic_slice_in_dim(zgate_proj, head_index * DV, DV, 1).astype(jnp.float32)
        log_gate = -lax.dynamic_slice_in_dim(gate_code, head_index, 1, 1)[:, 0].astype(jnp.float32) / 1048576.0
        beta_rows = lax.dynamic_slice_in_dim(beta_code, head_index, 1, 1)[:, 0].astype(jnp.float32) / 65536.0
        query_eff, local_out, transition, written = span_terms(query_rows.reshape(blocks, SPAN, DK), key_rows.reshape(blocks, SPAN, DK), value_rows.reshape(blocks, SPAN, DV), log_gate.reshape(blocks, SPAN), beta_rows.reshape(blocks, SPAN))

        def advance(state_now, step_items):
            query_block, local_block, trans_block, store_segment = step_items
            result = local_block + contract('cd,de->ce', query_block, state_now)
            state_now = contract('de,ef->df', trans_block, state_now) + store_segment
            return (state_now, result)
        start_state = jnp.zeros((DK, DV), jnp.float32)
        unused, core_out = lax.scan(advance, start_state, (query_eff, local_out, transition, written))
        core_out = core_out.reshape(SEQUENCE_LENGTH, DV)
        mean_square = lax.optimization_barrier(jnp.mean(core_out * core_out, -1, keepdims=True))
        normed = core_out * lax.rsqrt(mean_square + 1e-06) * norm_gain * jax.nn.silu(zgate_rows)
        return normed.astype(jnp.bfloat16)
    stacked = lax.map(one_head, jnp.arange(SHARD_OUTPUT_HEAD, dtype=jnp.int32))
    normed_all = jnp.transpose(stacked, (1, 0, 2)).reshape(SEQUENCE_LENGTH, SHARD_OUTPUT_HEAD * DV)
    return jnp.dot(normed_all.astype(jnp.float32), w_out.astype(jnp.float32), preferred_element_type=jnp.float32).astype(jnp.bfloat16)
```

```python
import functools
import jax
import jax.numpy as jnp
from jax import lax
from jax.experimental import pallas as pl
from jax.experimental.pallas import tpu as pltpu
from jax.sharding import PartitionSpec as P

DK = 128
DV = 128
KW = 4
CHUNK = 128
EDGE = 8
NN = (((1,), (0,)), ((), ()))
NT = (((1,), (1,)), ((), ()))
TN = (((0,), (0,)), ((), ()))


def split(x):
    high = x.astype(jnp.bfloat16)
    return high, (x - high.astype(jnp.float32)).astype(jnp.bfloat16)


def dot(a, b, dims=NN):
    return lax.dot_general(a, b, dims, preferred_element_type=jnp.float32)


def dot3(a, b, dims=NN):
    return dot(a[0], b[0], dims) + (dot(a[0], b[1], dims) + dot(a[1], b[0], dims))


def dot1(a, b, dims=NN):
    return dot(a[0], b[0], dims)


INV = dot3
MAIN = dot3


def unit_inverse(lower, rows, cols):
    eye = (rows == cols).astype(jnp.float32)
    near = jnp.where((rows >> 3) == (cols >> 3), -lower, 0.0)
    first = split(near)
    second = INV(first, first)
    power = split(second)
    total = eye + near
    total = total + INV(split(total), power)
    total = total + INV(split(total), split(INV(power, power)))
    width = 3
    while (1 << width) < CHUNK:
        pair = ((rows >> (width + 1)) == (cols >> (width + 1))) & ((rows >> width) != (cols >> width))
        off = split(jnp.where(pair, lower, 0.0))
        parts = split(total)
        total = total - INV(split(INV(parts, off)), parts)
        width += 1
    return total


def delta_kernel(key_heads, group, q_ref, k_ref, v_ref, rim_ref, taps_ref, gate_ref, core_ref, query_ref, state_ref, rows_ref, conv_ref, run_ref):
    step = pl.program_id(0)
    heads = key_heads * group
    rows = lax.broadcasted_iota(jnp.int32, (CHUNK, CHUNK), 0)
    cols = lax.broadcasted_iota(jnp.int32, (CHUNK, CHUNK), 1)
    qw, kw, vw = key_heads * DK, key_heads * DK, heads * DV

    @pl.when(step == 0)
    def _():
        rows_ref[0:EDGE, :] = rim_ref[...].astype(jnp.float32)
        for h in range(heads):
            run_ref[h] = jnp.concatenate([(rows == cols).astype(jnp.float32), jnp.zeros((DK, DV), jnp.float32)], 1)

    @pl.when(step > 0)
    def _():
        rows_ref[0:EDGE, :] = rows_ref[CHUNK : CHUNK + EDGE, :]

    rows_ref[EDGE:, 0:qw] = q_ref[...].astype(jnp.float32)
    rows_ref[EDGE:, qw : qw + kw] = k_ref[...].astype(jnp.float32)
    rows_ref[EDGE:, qw + kw :] = v_ref[...].astype(jnp.float32)
    for c in range(0, qw + kw + vw, 128):
        acc = jnp.zeros((CHUNK, 128), jnp.float32)
        for j in range(KW):
            start = EDGE - KW + 1 + j
            acc = acc + rows_ref[start : start + CHUNK, c : c + 128] * taps_ref[j : j + 1, c : c + 128].astype(jnp.float32)
        conv_ref[:, c : c + 128] = jax.nn.silu(acc).astype(jnp.bfloat16)

    gates = gate_ref[...]
    tri = (rows >= cols).astype(jnp.bfloat16)
    g1 = gates.astype(jnp.bfloat16)
    rest = gates - g1.astype(jnp.float32)
    g2 = rest.astype(jnp.bfloat16)
    g3 = (rest - g2.astype(jnp.float32)).astype(jnp.bfloat16)
    cum = dot(tri, g1) + (dot(tri, g2) + dot(tri, g3))
    cum_t = jnp.transpose(cum)
    strict = rows > cols
    incl = rows >= cols
    for kh in range(key_heads):
        q = conv_ref[:, kh * DK : (kh + 1) * DK]
        k_raw = conv_ref[:, qw + kh * DK : qw + (kh + 1) * DK].astype(jnp.float32)
        khat = k_raw / jnp.sqrt(jnp.sum(k_raw * k_raw, -1, keepdims=True) + 1e-06)
        ks = split(khat)
        gram = MAIN(ks, ks, NT)
        qk = dot(q, ks[0], NT) + dot(q, ks[1], NT)
        for r in range(group):
            h = kh * group + r
            col = cum[:, h : h + 1]
            row = cum_t[h : h + 1, :]
            beta = gates[:, heads + h : heads + h + 1]
            last = cum[CHUNK - 1 : CHUNK, h : h + 1]
            decay = jnp.exp(jnp.minimum(col - row, 0.0))
            lower = jnp.where(strict, beta * gram * decay, 0.0)
            inverse = split(unit_inverse(lower, rows, cols))
            grown = jnp.exp(col)
            v = conv_ref[:, qw + kw + h * DV : qw + kw + (h + 1) * DV].astype(jnp.float32)
            right = split(jnp.concatenate([khat * (beta * grown), v * beta], 1))
            wu = MAIN(inverse, right)
            scores = split(jnp.where(incl, qk * decay, 0.0))
            tail = split(khat * jnp.exp(last - col))
            run = run_ref[h]
            runs = split(run)
            y = jnp.concatenate([jnp.zeros((CHUNK, DK), jnp.float32), wu[:, DK:]], 1) - MAIN(split(wu[:, :DK]), runs)
            ys = split(y)
            out = grown * (dot(q, runs[0]) + dot(q, runs[1])) + MAIN(scores, ys)
            run_ref[h] = jnp.exp(last) * run + MAIN(tail, ys, TN)
            query_ref[:, h * DK : (h + 1) * DK] = out[:, :DK]
            core_ref[:, h * DV : (h + 1) * DV] = out[:, DK:]

    @pl.when(step == pl.num_programs(0) - 1)
    def _():
        state_ref[...] = run_ref[...].astype(state_ref.dtype)


def delta(q, k, v, rim, taps, gates, heads):
    length = q.shape[0]
    key_heads = q.shape[1] // DK
    width = q.shape[1] + k.shape[1] + v.shape[1]
    step_rows = lambda n: pl.BlockSpec((CHUNK, n), lambda i: (i, 0))
    whole = lambda *shape: pl.BlockSpec(shape, lambda i: (0,) * len(shape))
    return pl.pallas_call(
        functools.partial(delta_kernel, key_heads, heads // key_heads),
        grid=(length // CHUNK,),
        in_specs=[step_rows(q.shape[1]), step_rows(k.shape[1]), step_rows(v.shape[1]), whole(EDGE, width), whole(KW, width), step_rows(gates.shape[1])],
        out_specs=[step_rows(heads * DV), step_rows(heads * DK), whole(heads, DK, DK + DV)],
        out_shape=[
            jax.ShapeDtypeStruct((length, heads * DV), jnp.float32),
            jax.ShapeDtypeStruct((length, heads * DK), jnp.float32),
            jax.ShapeDtypeStruct((heads, DK, DK + DV), jnp.bfloat16),
        ],
        scratch_shapes=[
            pltpu.VMEM((CHUNK + EDGE, width), jnp.float32),
            pltpu.VMEM((CHUNK, width), jnp.bfloat16),
            pltpu.VMEM((heads, DK, DK + DV), jnp.float32),
        ],
        cost_estimate=pl.CostEstimate(flops=6 * 10**9, bytes_accessed=8 * 10**6, transcendentals=10**6),
        name="delta",
    )(q, k, v, rim, taps, gates)


def finish_kernel(count, heads, core_ref, query_ref, z_ref, maps_ref, gain_ref, out_ref, state_ref):
    mine = lax.axis_index("ctx")

    @pl.when(pl.program_id(0) == 0)
    def _():
        state_ref[...] = jnp.zeros_like(state_ref)

        def hop(p, carry):
            @pl.when(p < mine)
            def _():
                for h in range(heads):
                    s = split(state_ref[h])
                    trans = maps_ref[p, h, :, :DK]
                    state_ref[h] = dot(trans, s[0]) + dot(trans, s[1]) + maps_ref[p, h, :, DK:].astype(jnp.float32)

            return carry

        lax.fori_loop(0, count - 1, hop, 0)

    for h in range(heads):
        span = slice(h * DV, (h + 1) * DV)
        core = core_ref[:, span] + MAIN(split(query_ref[:, span]), split(state_ref[h]))
        z = z_ref[:, span].astype(jnp.float32)
        mean = jnp.mean(core * core, -1, keepdims=True)
        out_ref[:, span] = (core * lax.rsqrt(mean + 1e-06) * gain_ref[...] * jax.nn.silu(z)).astype(jnp.bfloat16)


def finish(core, query, z, maps, gain):
    length, wide = core.shape
    count, heads = maps.shape[:2]
    tile = min(256, length)
    step_rows = pl.BlockSpec((tile, wide), lambda i: (i, 0))
    return pl.pallas_call(
        functools.partial(finish_kernel, count, heads),
        grid=(length // tile,),
        in_specs=[step_rows, step_rows, step_rows, pl.BlockSpec(maps.shape, lambda i: (0, 0, 0, 0)), pl.BlockSpec((1, DV), lambda i: (0, 0))],
        out_specs=step_rows,
        out_shape=jax.ShapeDtypeStruct((length, wide), jnp.bfloat16),
        scratch_shapes=[pltpu.VMEM((heads, DK, DV), jnp.float32)],
        cost_estimate=pl.CostEstimate(flops=10**9, bytes_accessed=8 * 10**6, transcendentals=10**6),
        name="finish",
    )(core, query, z, maps, gain)


def shards(activations, w_query, w_key, w_value, w_zgate, conv_query, conv_key, conv_value, gate_code, beta_code, norm_gain, w_out):
    count = lax.axis_size("ctx")
    gathered = lax.all_gather(activations, "head", axis=0, tiled=True)
    length = gathered.shape[0]
    edge = lax.ppermute(gathered[length - EDGE :], "ctx", [(i, i + 1) for i in range(count - 1)])
    weights = [lax.all_gather(w, "ctx", axis=0, tiled=True) for w in (w_query, w_key, w_value, w_zgate)]
    project = lambda x, w: jnp.dot(x, w, preferred_element_type=jnp.float32).astype(jnp.bfloat16)
    q, k, v, z = [project(gathered, w) for w in weights]
    rim = jnp.concatenate([project(edge, w) for w in weights[:3]], 1)
    heads = gate_code.shape[1]
    gates = jnp.concatenate(
        [
            -gate_code.astype(jnp.float32) / 1048576.0,
            beta_code.astype(jnp.float32) / 65536.0,
            jnp.zeros((length, 128 - 2 * heads), jnp.float32),
        ],
        1,
    )
    taps = jnp.concatenate([conv_query, conv_key, conv_value], 1)
    core, query, state = delta(q, k, v, rim, taps, gates, heads)
    maps = lax.all_gather(state, "ctx", axis=0)
    normed = finish(core, query, z, maps, norm_gain.reshape(1, DV))
    out_weight = lax.all_gather(w_out, "ctx", axis=1, tiled=True)
    mixed = jnp.dot(normed, out_weight, preferred_element_type=jnp.float32).astype(jnp.bfloat16)
    return lax.psum_scatter(mixed, "head", scatter_dimension=0, tiled=True)


def solution(mesh):
    return jax.shard_map(
        shards,
        mesh=mesh,
        in_specs=(
            P(("ctx", "head"), None),
            P("ctx", "head"),
            P("ctx", "head"),
            P("ctx", "head"),
            P("ctx", "head"),
            P(None, "head"),
            P(None, "head"),
            P(None, "head"),
            P("ctx", "head"),
            P("ctx", "head"),
            P(),
            P("head", "ctx"),
        ),
        out_specs=P(("ctx", "head"), None),
        check_vma=False,
    )
```

```python
import functools
import jax
import jax.numpy as jnp
from jax import lax
from jax.experimental import pallas as pl
from jax.experimental.pallas import tpu as pltpu
from jax.sharding import PartitionSpec as P

DK = 128
DV = 128
KW = 4
CHUNK = 128
EDGE = 8
SUBS = 2
NN = (((1,), (0,)), ((), ()))
NT = (((1,), (1,)), ((), ()))
TN = (((0,), (0,)), ((), ()))


def split(x):
    high = x.astype(jnp.bfloat16)
    return high, (x - high.astype(jnp.float32)).astype(jnp.bfloat16)


def dot(a, b, dims=NN):
    return lax.dot_general(a, b, dims, preferred_element_type=jnp.float32)


def dot3(a, b, dims=NN):
    return dot(a[0], b[0], dims) + (dot(a[0], b[1], dims) + dot(a[1], b[0], dims))


def dot1(a, b, dims=NN):
    return dot(a[0], b[0], dims)


INV = dot3
MAIN = dot3


def unit_inverse(lower, rows, cols):
    eye = (rows == cols).astype(jnp.float32)
    near = jnp.where((rows >> 3) == (cols >> 3), -lower, 0.0)
    first = split(near)
    second = INV(first, first)
    power = split(second)
    total = eye + near
    total = total + INV(split(total), power)
    total = total + INV(split(total), split(INV(power, power)))
    width = 3
    while (1 << width) < CHUNK:
        pair = ((rows >> (width + 1)) == (cols >> (width + 1))) & ((rows >> width) != (cols >> width))
        off = split(jnp.where(pair, lower, 0.0))
        parts = split(total)
        total = total - INV(split(INV(parts, off)), parts)
        width += 1
    return total


def delta_kernel(key_heads, group, in_ref, rim_ref, taps_ref, gate_ref, core_ref, query_ref, state_ref, rows_ref, conv_ref, run_ref):
    step = pl.program_id(0)
    heads = key_heads * group
    rows = lax.broadcasted_iota(jnp.int32, (CHUNK, CHUNK), 0)
    cols = lax.broadcasted_iota(jnp.int32, (CHUNK, CHUNK), 1)
    qw, kw, vw = key_heads * DK, key_heads * DK, heads * DV

    @pl.when(step == 0)
    def _():
        rows_ref[0:EDGE, :] = rim_ref[...].astype(jnp.float32)
        for h in range(heads):
            run_ref[h] = jnp.concatenate([(rows == cols).astype(jnp.float32), jnp.zeros((DK, DV), jnp.float32)], 1)

    @pl.when(step > 0)
    def _():
        rows_ref[0:EDGE, :] = rows_ref[CHUNK : CHUNK + EDGE, :]

    rows_ref[EDGE:, :] = in_ref[...].astype(jnp.float32)
    for c in range(0, qw + kw + vw, 128):
        acc = jnp.zeros((CHUNK, 128), jnp.float32)
        for j in range(KW):
            start = EDGE - KW + 1 + j
            acc = acc + rows_ref[start : start + CHUNK, c : c + 128] * taps_ref[j : j + 1, c : c + 128].astype(jnp.float32)
        conv_ref[:, c : c + 128] = jax.nn.silu(acc).astype(jnp.bfloat16)

    gates = gate_ref[...]
    tri = (rows >= cols).astype(jnp.bfloat16)
    g1 = gates.astype(jnp.bfloat16)
    rest = gates - g1.astype(jnp.float32)
    g2 = rest.astype(jnp.bfloat16)
    g3 = (rest - g2.astype(jnp.float32)).astype(jnp.bfloat16)
    cum = dot(tri, g1) + (dot(tri, g2) + dot(tri, g3))
    cum_t = jnp.transpose(cum)
    strict = rows > cols
    incl = rows >= cols
    for kh in range(key_heads):
        q = conv_ref[:, kh * DK : (kh + 1) * DK]
        k_raw = conv_ref[:, qw + kh * DK : qw + (kh + 1) * DK].astype(jnp.float32)
        khat = k_raw / jnp.sqrt(jnp.sum(k_raw * k_raw, -1, keepdims=True) + 1e-06)
        ks = split(khat)
        gram = MAIN(ks, ks, NT)
        qk = dot(q, ks[0], NT) + dot(q, ks[1], NT)
        for r in range(group):
            h = kh * group + r
            col = cum[:, h : h + 1]
            row = cum_t[h : h + 1, :]
            beta = gates[:, heads + h : heads + h + 1]
            last = cum[CHUNK - 1 : CHUNK, h : h + 1]
            decay = jnp.exp(jnp.minimum(col - row, 0.0))
            lower = jnp.where(strict, beta * gram * decay, 0.0)
            inverse = split(unit_inverse(lower, rows, cols))
            grown = jnp.exp(col)
            v = conv_ref[:, qw + kw + h * DV : qw + kw + (h + 1) * DV].astype(jnp.float32)
            right = split(jnp.concatenate([khat * (beta * grown), v * beta], 1))
            wu = MAIN(inverse, right)
            scores = split(jnp.where(incl, qk * decay, 0.0))
            tail = split(khat * jnp.exp(last - col))
            run = run_ref[h]
            runs = split(run)
            y = jnp.concatenate([jnp.zeros((CHUNK, DK), jnp.float32), wu[:, DK:]], 1) - MAIN(split(wu[:, :DK]), runs)
            ys = split(y)
            out = grown * (dot(q, runs[0]) + dot(q, runs[1])) + MAIN(scores, ys)
            run_ref[h] = jnp.exp(last) * run + MAIN(tail, ys, TN)
            query_ref[:, h * DK : (h + 1) * DK] = out[:, :DK]
            core_ref[:, h * DV : (h + 1) * DV] = out[:, DK:]

    @pl.when(step == pl.num_programs(0) - 1)
    def _():
        state_ref[...] = run_ref[...].astype(state_ref.dtype)


def delta(joined, rim, taps, gates, key_width, heads):
    length = joined.shape[0]
    key_heads = key_width // DK
    width = rim.shape[1]
    step_rows = lambda n: pl.BlockSpec((CHUNK, n), lambda i: (i, 0))
    whole = lambda *shape: pl.BlockSpec(shape, lambda i: (0,) * len(shape))
    return pl.pallas_call(
        functools.partial(delta_kernel, key_heads, heads // key_heads),
        grid=(length // CHUNK,),
        in_specs=[step_rows(width), whole(EDGE, width), whole(KW, width), step_rows(gates.shape[1])],
        out_specs=[step_rows(heads * DV), step_rows(heads * DK), whole(heads, DK, DK + DV)],
        out_shape=[
            jax.ShapeDtypeStruct((length, heads * DV), jnp.float32),
            jax.ShapeDtypeStruct((length, heads * DK), jnp.float32),
            jax.ShapeDtypeStruct((heads, DK, DK + DV), jnp.bfloat16),
        ],
        scratch_shapes=[
            pltpu.VMEM((CHUNK + EDGE, width), jnp.float32),
            pltpu.VMEM((CHUNK, width), jnp.bfloat16),
            pltpu.VMEM((heads, DK, DK + DV), jnp.float32),
        ],
        cost_estimate=pl.CostEstimate(flops=60 * 10**9, bytes_accessed=8 * 10**6, transcendentals=10**6),
        name="delta",
    )(joined, rim, taps, gates)


def finish_kernel(count, heads, core_ref, query_ref, z_ref, maps_ref, gain_ref, out_ref, state_ref):
    mine = lax.axis_index("ctx")

    @pl.when(pl.program_id(0) == 0)
    def _():
        state_ref[...] = jnp.zeros_like(state_ref)

        def hop(p, carry):
            @pl.when(p < mine)
            def _():
                for h in range(heads):
                    s = split(state_ref[h])
                    trans = maps_ref[p, h, :, :DK]
                    state_ref[h] = dot(trans, s[0]) + dot(trans, s[1]) + maps_ref[p, h, :, DK:].astype(jnp.float32)

            return carry

        lax.fori_loop(0, count - 1, hop, 0)

    for h in range(heads):
        span = slice(h * DV, (h + 1) * DV)
        core = core_ref[:, span] + MAIN(split(query_ref[:, span]), split(state_ref[h]))
        z = z_ref[:, span].astype(jnp.float32)
        mean = jnp.mean(core * core, -1, keepdims=True)
        out_ref[:, span] = (core * lax.rsqrt(mean + 1e-06) * gain_ref[...] * jax.nn.silu(z)).astype(jnp.bfloat16)


def finish(core, query, joined, maps, gain):
    length, wide = core.shape
    count, heads = maps.shape[:2]
    tile = min(256, length)
    step_rows = pl.BlockSpec((tile, wide), lambda i: (i, 0))
    return pl.pallas_call(
        functools.partial(finish_kernel, count, heads),
        grid=(length // tile,),
        in_specs=[step_rows, step_rows, pl.BlockSpec((tile, wide), lambda i: (i, joined.shape[1] // wide - 1)), pl.BlockSpec(maps.shape, lambda i: (0, 0, 0, 0)), pl.BlockSpec((1, DV), lambda i: (0, 0))],
        out_specs=step_rows,
        out_shape=jax.ShapeDtypeStruct((length, wide), jnp.bfloat16),
        scratch_shapes=[pltpu.VMEM((heads, DK, DV), jnp.float32)],
        cost_estimate=pl.CostEstimate(flops=10**9, bytes_accessed=8 * 10**6, transcendentals=10**6),
        name="finish",
    )(core, query, joined, maps, gain)


def ring_device(position, n):
    odd = lax.div(position, n // 2)
    return (1 - odd) * (2 * position) + odd * (2 * (n - 1 - position) + 1)


def gather_kernel(n, heads, act_ref, w_ref, act_out, w_out, act_tmp, w_tmp, local_sem, act_send, act_recv, ring_send, ring_recv):
    ctx, head = lax.axis_index("ctx"), lax.axis_index("head")
    odd = lax.rem(ctx, 2)
    position = (1 - odd) * lax.div(ctx, 2) + odd * (n - 1 - lax.div(ctx, 2))
    after = ring_device(lax.rem(position + 1, n), n)
    before = ring_device(lax.rem(position + n - 1, n), n)
    peers = [lax.rem(head + d, heads) for d in range(1, heads)]

    barrier = pltpu.get_barrier_semaphore()
    for other in (after, before):
        pl.semaphore_signal(barrier, inc=1, device_id=(other, head), device_id_type=pl.DeviceIdType.MESH)
    for peer in peers:
        pl.semaphore_signal(barrier, inc=1, device_id=(ctx, peer), device_id_type=pl.DeviceIdType.MESH)
    pl.semaphore_wait(barrier, heads + 1)

    piece = w_ref.shape[0] // (2 * SUBS)

    def hop(s, way, sub):
        offset = (way * SUBS + sub) * piece
        owner = ring_device(lax.rem(position + (n - s if way == 0 else s), n), n)
        place = w_out.at[owner, pl.ds(offset, piece)]
        return pltpu.make_async_remote_copy(
            src_ref=w_ref.at[pl.ds(offset, piece)] if s == 0 else place,
            dst_ref=place,
            send_sem=ring_send.at[s, way * SUBS + sub],
            recv_sem=ring_recv.at[s, way * SUBS + sub],
            device_id=(after if way == 0 else before, head),
            device_id_type=pl.DeviceIdType.MESH,
        )

    hops = [[hop(s, way, sub) for sub in range(SUBS) for way in range(2)] for s in range(n - 1)]
    for copy in hops[0]:
        copy.start()
    sends = [
        pltpu.make_async_remote_copy(
            src_ref=act_ref,
            dst_ref=act_out.at[head],
            send_sem=act_send.at[d],
            recv_sem=act_recv.at[d],
            device_id=(ctx, peer),
            device_id_type=pl.DeviceIdType.MESH,
        )
        for d, peer in enumerate(peers)
    ]
    for copy in sends:
        copy.start()
    take = [pltpu.make_async_copy(act_ref, act_tmp, local_sem.at[0]), pltpu.make_async_copy(w_ref, w_tmp, local_sem.at[1])]
    keep = [
        pltpu.make_async_copy(act_tmp, act_out.at[head], local_sem.at[2]),
        pltpu.make_async_copy(w_tmp, w_out.at[ctx], local_sem.at[3]),
    ]
    for copy in take:
        copy.start()
    for one, two in zip(take, keep):
        one.wait()
        two.start()
    for s in range(1, n - 1):
        for arrived, copy in zip(hops[s - 1], hops[s]):
            arrived.wait_recv()
            copy.start()
    for copy in hops[n - 2]:
        copy.wait_recv()
    for copy in sends:
        copy.wait_recv()
    for two in keep:
        two.wait()
    for copy in sends:
        copy.wait_send()
    for row in hops:
        for copy in row:
            copy.wait_send()


def gather_inputs(activations, weights):
    n, heads = lax.axis_size("ctx"), lax.axis_size("head")
    anywhere = pl.BlockSpec(memory_space=pl.ANY)
    act, w = pl.pallas_call(
        functools.partial(gather_kernel, n, heads),
        in_specs=[anywhere, anywhere],
        out_specs=[anywhere, anywhere],
        out_shape=[
            jax.ShapeDtypeStruct((heads,) + activations.shape, activations.dtype),
            jax.ShapeDtypeStruct((n,) + weights.shape, weights.dtype),
        ],
        scratch_shapes=[
            pltpu.VMEM(activations.shape, activations.dtype),
            pltpu.VMEM(weights.shape, weights.dtype),
            pltpu.SemaphoreType.DMA((4,)),
            pltpu.SemaphoreType.DMA((heads - 1,)),
            pltpu.SemaphoreType.DMA((heads - 1,)),
            pltpu.SemaphoreType.DMA((n - 1, 2 * SUBS)),
            pltpu.SemaphoreType.DMA((n - 1, 2 * SUBS)),
        ],
        compiler_params=pltpu.CompilerParams(collective_id=0, has_side_effects=True),
        name="gather_inputs",
    )(activations, weights)
    return act.reshape(-1, act.shape[-1]), w.reshape(-1, w.shape[-1])


def shards(activations, w_query, w_key, w_value, w_zgate, conv_query, conv_key, conv_value, gate_code, beta_code, norm_gain, w_out):
    count = lax.axis_size("ctx")
    gathered, weight = gather_inputs(activations, jnp.concatenate([w_query, w_key, w_value, w_zgate], 1))
    length = gathered.shape[0]
    conv_width = conv_query.shape[1] + conv_key.shape[1] + conv_value.shape[1]
    project = lambda x, w: jnp.dot(x, w, preferred_element_type=jnp.float32).astype(jnp.bfloat16)
    edge = lax.ppermute(gathered[length - EDGE :], "ctx", [(i, i + 1) for i in range(count - 1)])
    rim = project(edge, weight[:, :conv_width])
    joined = project(gathered, weight)
    heads = gate_code.shape[1]
    gates = jnp.concatenate(
        [
            -gate_code.astype(jnp.float32) / 1048576.0,
            beta_code.astype(jnp.float32) / 65536.0,
            jnp.zeros((length, 128 - 2 * heads), jnp.float32),
        ],
        1,
    )
    taps = jnp.concatenate([conv_query, conv_key, conv_value], 1)
    w_out, joined = lax.optimization_barrier((w_out, joined))
    out_weight = lax.all_gather(w_out, "ctx", axis=1, tiled=True)
    core, query, state = delta(joined, rim, taps, gates, conv_query.shape[1], heads)
    maps = lax.all_gather(state, "ctx", axis=0)
    normed = finish(core, query, joined, maps, norm_gain.reshape(1, DV))
    mixed = jnp.dot(normed, out_weight, preferred_element_type=jnp.float32).astype(jnp.bfloat16)
    return lax.psum_scatter(mixed, "head", scatter_dimension=0, tiled=True)


def solution(mesh):
    return jax.shard_map(
        shards,
        mesh=mesh,
        in_specs=(
            P(("ctx", "head"), None),
            P("ctx", "head"),
            P("ctx", "head"),
            P("ctx", "head"),
            P("ctx", "head"),
            P(None, "head"),
            P(None, "head"),
            P(None, "head"),
            P("ctx", "head"),
            P("ctx", "head"),
            P(),
            P("head", "ctx"),
        ),
        out_specs=P(("ctx", "head"), None),
        check_vma=False,
    )
```

```python
import functools
import jax
import jax.numpy as jnp
from jax import lax
from jax.experimental import pallas as pl
from jax.experimental.pallas import tpu as pltpu
from jax.sharding import PartitionSpec as P

DK = 128
DV = 128
KW = 4
CHUNK = 128
EDGE = 8
SUBS = 2
NN = (((1,), (0,)), ((), ()))
NT = (((1,), (1,)), ((), ()))
TN = (((0,), (0,)), ((), ()))


def split(x):
    high = x.astype(jnp.bfloat16)
    return high, (x - high.astype(jnp.float32)).astype(jnp.bfloat16)


def dot(a, b, dims=NN):
    return lax.dot_general(a, b, dims, preferred_element_type=jnp.float32)


def dot3(a, b, dims=NN):
    return dot(a[0], b[0], dims) + (dot(a[0], b[1], dims) + dot(a[1], b[0], dims))


def dot1(a, b, dims=NN):
    return dot(a[0], b[0], dims)


INV = dot3
MAIN = dot3


def unit_inverses(lowers, rows, cols):
    eye = (rows == cols).astype(jnp.float32)
    near = [jnp.where((rows >> 3) == (cols >> 3), -x, 0.0) for x in lowers]
    first = [split(x) for x in near]
    second = [split(INV(x, x)) for x in first]
    totals = [eye + x for x in near]
    steps = [INV(split(t), p) for t, p in zip(totals, second)]
    fourth = [split(INV(p, p)) for p in second]
    totals = [t + x for t, x in zip(totals, steps)]
    steps = [INV(split(t), p) for t, p in zip(totals, fourth)]
    totals = [t + x for t, x in zip(totals, steps)]
    width = 3
    while (1 << width) < CHUNK:
        size = 1 << width
        pair = ((rows >> (width + 1)) == (cols >> (width + 1))) & ((rows >> width) != (cols >> width))
        starts = range(size, CHUNK, 2 * size)
        off = [split(jnp.where(pair, x, 0.0)) for x in lowers]
        parts = [split(t) for t in totals]
        odd = [split(jnp.concatenate([t[i : i + size] for i in starts], 0)) for t in totals]
        left = [split(INV(o, c)) for o, c in zip(odd, off)]
        change = [INV(x, t) for x, t in zip(left, parts)]
        joined = []
        for t, c in zip(totals, change):
            pieces = []
            for n, i in enumerate(starts):
                pieces += [t[i - size : i], t[i : i + size] - c[n * size : (n + 1) * size]]
            joined.append(jnp.concatenate(pieces, 0))
        totals = joined
        width += 1
    return totals


def delta_kernel(key_heads, group, in_ref, rim_ref, taps_ref, gate_ref, core_ref, query_ref, state_ref, rows_ref, conv_ref, run_ref):
    step = pl.program_id(0)
    heads = key_heads * group
    rows = lax.broadcasted_iota(jnp.int32, (CHUNK, CHUNK), 0)
    cols = lax.broadcasted_iota(jnp.int32, (CHUNK, CHUNK), 1)
    qw, kw, vw = key_heads * DK, key_heads * DK, heads * DV

    @pl.when(step == 0)
    def _():
        rows_ref[0:EDGE, :] = rim_ref[...].astype(jnp.float32)
        for h in range(heads):
            run_ref[h] = jnp.concatenate([(rows == cols).astype(jnp.float32), jnp.zeros((DK, DV), jnp.float32)], 1)

    @pl.when(step > 0)
    def _():
        rows_ref[0:EDGE, :] = rows_ref[CHUNK : CHUNK + EDGE, :]

    rows_ref[EDGE:, :] = in_ref[...].astype(jnp.float32)
    for c in range(0, qw + kw + vw, 128):
        acc = jnp.zeros((CHUNK, 128), jnp.float32)
        for j in range(KW):
            start = EDGE - KW + 1 + j
            acc = acc + rows_ref[start : start + CHUNK, c : c + 128] * taps_ref[j : j + 1, c : c + 128].astype(jnp.float32)
        conv_ref[:, c : c + 128] = jax.nn.silu(acc).astype(jnp.bfloat16)

    gates = gate_ref[...]
    tri = (rows >= cols).astype(jnp.bfloat16)
    g1 = gates.astype(jnp.bfloat16)
    rest = gates - g1.astype(jnp.float32)
    g2 = rest.astype(jnp.bfloat16)
    g3 = (rest - g2.astype(jnp.float32)).astype(jnp.bfloat16)
    cum = dot(tri, g1) + (dot(tri, g2) + dot(tri, g3))
    cum_t = jnp.transpose(cum)
    strict = rows > cols
    incl = rows >= cols
    qs = [conv_ref[:, i * DK : (i + 1) * DK] for i in range(key_heads)]
    raws = [conv_ref[:, qw + i * DK : qw + (i + 1) * DK].astype(jnp.float32) for i in range(key_heads)]
    khats = [x / jnp.sqrt(jnp.sum(x * x, -1, keepdims=True) + 1e-06) for x in raws]
    ks = [split(x) for x in khats]
    grams = [MAIN(x, x, NT) for x in ks]
    qks = [dot(q, k[0], NT) + dot(q, k[1], NT) for q, k in zip(qs, ks)]
    every = range(heads)
    col = [cum[:, h : h + 1] for h in every]
    beta = [gates[:, heads + h : heads + h + 1] for h in every]
    last = [cum[CHUNK - 1 : CHUNK, h : h + 1] for h in every]
    decay = [jnp.exp(jnp.minimum(col[h] - cum_t[h : h + 1, :], 0.0)) for h in every]
    grown = [jnp.exp(col[h]) for h in every]
    lowers = [jnp.where(strict, beta[h] * grams[h // group] * decay[h], 0.0) for h in every]
    inverses = [split(x) for x in unit_inverses(lowers, rows, cols)]
    vs = [conv_ref[:, qw + kw + h * DV : qw + kw + (h + 1) * DV].astype(jnp.float32) for h in every]
    right = [split(jnp.concatenate([khats[h // group] * (beta[h] * grown[h]), vs[h] * beta[h]], 1)) for h in every]
    wu = [MAIN(inverses[h], right[h]) for h in every]
    runs = [split(run_ref[h]) for h in every]
    back = [MAIN(split(wu[h][:, :DK]), runs[h]) for h in every]
    blank = jnp.zeros((CHUNK, DK), jnp.float32)
    ys = [split(jnp.concatenate([blank, wu[h][:, DK:]], 1) - back[h]) for h in every]
    scores = [split(jnp.where(incl, qks[h // group] * decay[h], 0.0)) for h in every]
    tails = [split(khats[h // group] * jnp.exp(last[h] - col[h])) for h in every]
    grow = [MAIN(tails[h], ys[h], TN) for h in every]
    seen = [dot(qs[h // group], runs[h][0]) + dot(qs[h // group], runs[h][1]) for h in every]
    mixed = [MAIN(scores[h], ys[h]) for h in every]
    for h in every:
        run_ref[h] = jnp.exp(last[h]) * run_ref[h] + grow[h]
        out = grown[h] * seen[h] + mixed[h]
        query_ref[:, h * DK : (h + 1) * DK] = out[:, :DK]
        core_ref[:, h * DV : (h + 1) * DV] = out[:, DK:]

    @pl.when(step == pl.num_programs(0) - 1)
    def _():
        state_ref[...] = run_ref[...].astype(state_ref.dtype)


def delta(joined, rim, taps, gates, key_width, heads):
    length = joined.shape[0]
    key_heads = key_width // DK
    width = rim.shape[1]
    step_rows = lambda n: pl.BlockSpec((CHUNK, n), lambda i: (i, 0))
    whole = lambda *shape: pl.BlockSpec(shape, lambda i: (0,) * len(shape))
    return pl.pallas_call(
        functools.partial(delta_kernel, key_heads, heads // key_heads),
        grid=(length // CHUNK,),
        in_specs=[step_rows(width), whole(EDGE, width), whole(KW, width), step_rows(gates.shape[1])],
        out_specs=[step_rows(heads * DV), step_rows(heads * DK), whole(heads, DK, DK + DV)],
        out_shape=[
            jax.ShapeDtypeStruct((length, heads * DV), jnp.float32),
            jax.ShapeDtypeStruct((length, heads * DK), jnp.float32),
            jax.ShapeDtypeStruct((heads, DK, DK + DV), jnp.bfloat16),
        ],
        scratch_shapes=[
            pltpu.VMEM((CHUNK + EDGE, width), jnp.float32),
            pltpu.VMEM((CHUNK, width), jnp.bfloat16),
            pltpu.VMEM((heads, DK, DK + DV), jnp.float32),
        ],
        cost_estimate=pl.CostEstimate(flops=60 * 10**9, bytes_accessed=8 * 10**6, transcendentals=10**6),
        name="delta",
    )(joined, rim, taps, gates)


def finish_kernel(count, heads, core_ref, query_ref, z_ref, maps_ref, gain_ref, out_ref, state_ref):
    mine = lax.axis_index("ctx")

    @pl.when(pl.program_id(0) == 0)
    def _():
        state_ref[...] = jnp.zeros_like(state_ref)

        def hop(p, carry):
            @pl.when(p < mine)
            def _():
                for h in range(heads):
                    s = split(state_ref[h])
                    trans = maps_ref[p, h, :, :DK]
                    state_ref[h] = dot(trans, s[0]) + dot(trans, s[1]) + maps_ref[p, h, :, DK:].astype(jnp.float32)

            return carry

        lax.fori_loop(0, count - 1, hop, 0)

    for h in range(heads):
        span = slice(h * DV, (h + 1) * DV)
        core = core_ref[:, span] + MAIN(split(query_ref[:, span]), split(state_ref[h]))
        z = z_ref[:, span].astype(jnp.float32)
        mean = jnp.mean(core * core, -1, keepdims=True)
        out_ref[:, span] = (core * lax.rsqrt(mean + 1e-06) * gain_ref[...] * jax.nn.silu(z)).astype(jnp.bfloat16)


def finish(core, query, joined, maps, gain):
    length, wide = core.shape
    count, heads = maps.shape[:2]
    tile = min(256, length)
    step_rows = pl.BlockSpec((tile, wide), lambda i: (i, 0))
    return pl.pallas_call(
        functools.partial(finish_kernel, count, heads),
        grid=(length // tile,),
        in_specs=[step_rows, step_rows, pl.BlockSpec((tile, wide), lambda i: (i, joined.shape[1] // wide - 1)), pl.BlockSpec(maps.shape, lambda i: (0, 0, 0, 0)), pl.BlockSpec((1, DV), lambda i: (0, 0))],
        out_specs=step_rows,
        out_shape=jax.ShapeDtypeStruct((length, wide), jnp.bfloat16),
        scratch_shapes=[pltpu.VMEM((heads, DK, DV), jnp.float32)],
        cost_estimate=pl.CostEstimate(flops=10**9, bytes_accessed=8 * 10**6, transcendentals=10**6),
        name="finish",
    )(core, query, joined, maps, gain)


def ring_device(position, n):
    odd = lax.div(position, n // 2)
    return (1 - odd) * (2 * position) + odd * (2 * (n - 1 - position) + 1)


def gather_kernel(n, heads, act_ref, w_ref, act_out, w_out, act_tmp, w_tmp, local_sem, act_send, act_recv, ring_send, ring_recv):
    ctx, head = lax.axis_index("ctx"), lax.axis_index("head")
    odd = lax.rem(ctx, 2)
    position = (1 - odd) * lax.div(ctx, 2) + odd * (n - 1 - lax.div(ctx, 2))
    after = ring_device(lax.rem(position + 1, n), n)
    before = ring_device(lax.rem(position + n - 1, n), n)
    peers = [lax.rem(head + d, heads) for d in range(1, heads)]

    barrier = pltpu.get_barrier_semaphore()
    for other in (after, before):
        pl.semaphore_signal(barrier, inc=1, device_id=(other, head), device_id_type=pl.DeviceIdType.MESH)
    for peer in peers:
        pl.semaphore_signal(barrier, inc=1, device_id=(ctx, peer), device_id_type=pl.DeviceIdType.MESH)
    pl.semaphore_wait(barrier, heads + 1)

    piece = w_ref.shape[0] // (2 * SUBS)

    def hop(s, way, sub):
        offset = (way * SUBS + sub) * piece
        owner = ring_device(lax.rem(position + (n - s if way == 0 else s), n), n)
        place = w_out.at[owner, pl.ds(offset, piece)]
        return pltpu.make_async_remote_copy(
            src_ref=w_ref.at[pl.ds(offset, piece)] if s == 0 else place,
            dst_ref=place,
            send_sem=ring_send.at[s, way * SUBS + sub],
            recv_sem=ring_recv.at[s, way * SUBS + sub],
            device_id=(after if way == 0 else before, head),
            device_id_type=pl.DeviceIdType.MESH,
        )

    hops = [[hop(s, way, sub) for sub in range(SUBS) for way in range(2)] for s in range(n - 1)]
    for copy in hops[0]:
        copy.start()
    sends = [
        pltpu.make_async_remote_copy(
            src_ref=act_ref,
            dst_ref=act_out.at[head],
            send_sem=act_send.at[d],
            recv_sem=act_recv.at[d],
            device_id=(ctx, peer),
            device_id_type=pl.DeviceIdType.MESH,
        )
        for d, peer in enumerate(peers)
    ]
    for copy in sends:
        copy.start()
    take = [pltpu.make_async_copy(act_ref, act_tmp, local_sem.at[0]), pltpu.make_async_copy(w_ref, w_tmp, local_sem.at[1])]
    keep = [
        pltpu.make_async_copy(act_tmp, act_out.at[head], local_sem.at[2]),
        pltpu.make_async_copy(w_tmp, w_out.at[ctx], local_sem.at[3]),
    ]
    for copy in take:
        copy.start()
    for one, two in zip(take, keep):
        one.wait()
        two.start()
    for s in range(1, n - 1):
        for arrived, copy in zip(hops[s - 1], hops[s]):
            arrived.wait_recv()
            copy.start()
    for copy in hops[n - 2]:
        copy.wait_recv()
    for copy in sends:
        copy.wait_recv()
    for two in keep:
        two.wait()
    for copy in sends:
        copy.wait_send()
    for row in hops:
        for copy in row:
            copy.wait_send()


def gather_inputs(activations, weights):
    n, heads = lax.axis_size("ctx"), lax.axis_size("head")
    anywhere = pl.BlockSpec(memory_space=pl.ANY)
    act, w = pl.pallas_call(
        functools.partial(gather_kernel, n, heads),
        in_specs=[anywhere, anywhere],
        out_specs=[anywhere, anywhere],
        out_shape=[
            jax.ShapeDtypeStruct((heads,) + activations.shape, activations.dtype),
            jax.ShapeDtypeStruct((n,) + weights.shape, weights.dtype),
        ],
        scratch_shapes=[
            pltpu.VMEM(activations.shape, activations.dtype),
            pltpu.VMEM(weights.shape, weights.dtype),
            pltpu.SemaphoreType.DMA((4,)),
            pltpu.SemaphoreType.DMA((heads - 1,)),
            pltpu.SemaphoreType.DMA((heads - 1,)),
            pltpu.SemaphoreType.DMA((n - 1, 2 * SUBS)),
            pltpu.SemaphoreType.DMA((n - 1, 2 * SUBS)),
        ],
        compiler_params=pltpu.CompilerParams(collective_id=0, has_side_effects=True),
        name="gather_inputs",
    )(activations, weights)
    return act.reshape(-1, act.shape[-1]), w.reshape(-1, w.shape[-1])


def shards(activations, w_query, w_key, w_value, w_zgate, conv_query, conv_key, conv_value, gate_code, beta_code, norm_gain, w_out):
    count = lax.axis_size("ctx")
    gathered, weight = gather_inputs(activations, jnp.concatenate([w_query, w_key, w_value, w_zgate], 1))
    w_out, gathered = lax.optimization_barrier((w_out, gathered))
    out_weight = lax.all_gather(w_out, "ctx", axis=1, tiled=True)
    length = gathered.shape[0]
    conv_width = conv_query.shape[1] + conv_key.shape[1] + conv_value.shape[1]
    project = lambda x, w: jnp.dot(x, w, preferred_element_type=jnp.float32).astype(jnp.bfloat16)
    edge = lax.ppermute(gathered[length - EDGE :], "ctx", [(i, i + 1) for i in range(count - 1)])
    rim = project(edge, weight[:, :conv_width])
    joined = project(gathered, weight)
    heads = gate_code.shape[1]
    gates = jnp.concatenate(
        [
            -gate_code.astype(jnp.float32) / 1048576.0,
            beta_code.astype(jnp.float32) / 65536.0,
            jnp.zeros((length, 128 - 2 * heads), jnp.float32),
        ],
        1,
    )
    taps = jnp.concatenate([conv_query, conv_key, conv_value], 1)
    core, query, state = delta(joined, rim, taps, gates, conv_query.shape[1], heads)
    state, out_weight = lax.optimization_barrier((state, out_weight))
    maps = lax.all_gather(state, "ctx", axis=0)
    normed = finish(core, query, joined, maps, norm_gain.reshape(1, DV))
    mixed = jnp.dot(normed, out_weight, preferred_element_type=jnp.float32).astype(jnp.bfloat16)
    return lax.psum_scatter(mixed, "head", scatter_dimension=0, tiled=True)


def solution(mesh):
    return jax.shard_map(
        shards,
        mesh=mesh,
        in_specs=(
            P(("ctx", "head"), None),
            P("ctx", "head"),
            P("ctx", "head"),
            P("ctx", "head"),
            P("ctx", "head"),
            P(None, "head"),
            P(None, "head"),
            P(None, "head"),
            P("ctx", "head"),
            P("ctx", "head"),
            P(),
            P("head", "ctx"),
        ),
        out_specs=P(("ctx", "head"), None),
        check_vma=False,
    )
```

```python
import functools
import jax
import jax.numpy as jnp
from jax import lax
from jax.experimental import pallas as pl
from jax.experimental.pallas import tpu as pltpu
from jax.sharding import PartitionSpec as P

DK = 128
DV = 128
KW = 4
CHUNK = 128
EDGE = 8
SUBS = 2
NN = (((1,), (0,)), ((), ()))
NT = (((1,), (1,)), ((), ()))
TN = (((0,), (0,)), ((), ()))


def split(x):
    high = x.astype(jnp.bfloat16)
    return high, (x - high.astype(jnp.float32)).astype(jnp.bfloat16)


def dot(a, b, dims=NN):
    return lax.dot_general(a, b, dims, preferred_element_type=jnp.float32)


def dot3(a, b, dims=NN):
    return dot(a[0], b[0], dims) + (dot(a[0], b[1], dims) + dot(a[1], b[0], dims))


def dot1(a, b, dims=NN):
    return dot(a[0], b[0], dims)


INV = dot3
MAIN = dot3


def unit_inverses(lowers, rows, cols):
    eye = (rows == cols).astype(jnp.float32)
    near = [jnp.where((rows >> 3) == (cols >> 3), -x, 0.0) for x in lowers]
    first = [split(x) for x in near]
    second = [split(INV(x, x)) for x in first]
    totals = [eye + x for x in near]
    steps = [INV(split(t), p) for t, p in zip(totals, second)]
    fourth = [split(INV(p, p)) for p in second]
    totals = [t + x for t, x in zip(totals, steps)]
    steps = [INV(split(t), p) for t, p in zip(totals, fourth)]
    totals = [t + x for t, x in zip(totals, steps)]
    width = 3
    while (1 << width) < CHUNK:
        size = 1 << width
        pair = ((rows >> (width + 1)) == (cols >> (width + 1))) & ((rows >> width) != (cols >> width))
        starts = range(size, CHUNK, 2 * size)
        off = [split(jnp.where(pair, x, 0.0)) for x in lowers]
        parts = [split(t) for t in totals]
        odd = [split(jnp.concatenate([t[i : i + size] for i in starts], 0)) for t in totals]
        left = [split(INV(o, c)) for o, c in zip(odd, off)]
        change = [INV(x, t) for x, t in zip(left, parts)]
        joined = []
        for t, c in zip(totals, change):
            pieces = []
            for n, i in enumerate(starts):
                pieces += [t[i - size : i], t[i : i + size] - c[n * size : (n + 1) * size]]
            joined.append(jnp.concatenate(pieces, 0))
        totals = joined
        width += 1
    return totals


def delta_kernel(key_heads, group, in_ref, rim_ref, taps_ref, gate_ref, core_ref, query_ref, state_ref, rows_ref, conv_ref, run_ref):
    step = pl.program_id(0)
    heads = key_heads * group
    rows = lax.broadcasted_iota(jnp.int32, (CHUNK, CHUNK), 0)
    cols = lax.broadcasted_iota(jnp.int32, (CHUNK, CHUNK), 1)
    qw, kw, vw = key_heads * DK, key_heads * DK, heads * DV

    @pl.when(step == 0)
    def _():
        rows_ref[0:EDGE, :] = rim_ref[...].astype(jnp.float32)
        for h in range(heads):
            run_ref[h] = jnp.concatenate([(rows == cols).astype(jnp.float32), jnp.zeros((DK, DV), jnp.float32)], 1)

    @pl.when(step > 0)
    def _():
        rows_ref[0:EDGE, :] = rows_ref[CHUNK : CHUNK + EDGE, :]

    rows_ref[EDGE:, :] = in_ref[...].astype(jnp.float32)
    for c in range(0, qw + kw + vw, 128):
        acc = jnp.zeros((CHUNK, 128), jnp.float32)
        for j in range(KW):
            start = EDGE - KW + 1 + j
            acc = acc + rows_ref[start : start + CHUNK, c : c + 128] * taps_ref[j : j + 1, c : c + 128].astype(jnp.float32)
        conv_ref[:, c : c + 128] = jax.nn.silu(acc).astype(jnp.bfloat16)

    gates = gate_ref[...]
    tri = (rows >= cols).astype(jnp.bfloat16)
    g1 = gates.astype(jnp.bfloat16)
    rest = gates - g1.astype(jnp.float32)
    g2 = rest.astype(jnp.bfloat16)
    g3 = (rest - g2.astype(jnp.float32)).astype(jnp.bfloat16)
    cum = dot(tri, g1) + (dot(tri, g2) + dot(tri, g3))
    cum_t = jnp.transpose(cum)
    strict = rows > cols
    incl = rows >= cols
    qs = [conv_ref[:, i * DK : (i + 1) * DK] for i in range(key_heads)]
    raws = [conv_ref[:, qw + i * DK : qw + (i + 1) * DK].astype(jnp.float32) for i in range(key_heads)]
    khats = [x / jnp.sqrt(jnp.sum(x * x, -1, keepdims=True) + 1e-06) for x in raws]
    ks = [split(x) for x in khats]
    grams = [MAIN(x, x, NT) for x in ks]
    qks = [dot(q, k[0], NT) + dot(q, k[1], NT) for q, k in zip(qs, ks)]
    every = range(heads)
    col = [cum[:, h : h + 1] for h in every]
    beta = [gates[:, heads + h : heads + h + 1] for h in every]
    last = [cum[CHUNK - 1 : CHUNK, h : h + 1] for h in every]
    decay = [jnp.exp(jnp.minimum(col[h] - cum_t[h : h + 1, :], 0.0)) for h in every]
    grown = [jnp.exp(col[h]) for h in every]
    lowers = [jnp.where(strict, beta[h] * grams[h // group] * decay[h], 0.0) for h in every]
    inverses = [split(x) for x in unit_inverses(lowers, rows, cols)]
    vs = [conv_ref[:, qw + kw + h * DV : qw + kw + (h + 1) * DV].astype(jnp.float32) for h in every]
    right = [split(jnp.concatenate([khats[h // group] * (beta[h] * grown[h]), vs[h] * beta[h]], 1)) for h in every]
    wu = [MAIN(inverses[h], right[h]) for h in every]
    runs = [split(run_ref[h]) for h in every]
    back = [MAIN(split(wu[h][:, :DK]), runs[h]) for h in every]
    blank = jnp.zeros((CHUNK, DK), jnp.float32)
    ys = [split(jnp.concatenate([blank, wu[h][:, DK:]], 1) - back[h]) for h in every]
    scores = [split(jnp.where(incl, qks[h // group] * decay[h], 0.0)) for h in every]
    tails = [split(khats[h // group] * jnp.exp(last[h] - col[h])) for h in every]
    grow = [MAIN(tails[h], ys[h], TN) for h in every]
    seen = [dot(qs[h // group], runs[h][0]) + dot(qs[h // group], runs[h][1]) for h in every]
    mixed = [MAIN(scores[h], ys[h]) for h in every]
    for h in every:
        run_ref[h] = jnp.exp(last[h]) * run_ref[h] + grow[h]
        out = grown[h] * seen[h] + mixed[h]
        query_ref[:, h * DK : (h + 1) * DK] = out[:, :DK]
        core_ref[:, h * DV : (h + 1) * DV] = out[:, DK:]

    @pl.when(step == pl.num_programs(0) - 1)
    def _():
        state_ref[...] = run_ref[...].astype(state_ref.dtype)


def delta(joined, rim, taps, gates, key_width, heads):
    length = joined.shape[0]
    key_heads = key_width // DK
    width = rim.shape[1]
    step_rows = lambda n: pl.BlockSpec((CHUNK, n), lambda i: (i, 0))
    whole = lambda *shape: pl.BlockSpec(shape, lambda i: (0,) * len(shape))
    return pl.pallas_call(
        functools.partial(delta_kernel, key_heads, heads // key_heads),
        grid=(length // CHUNK,),
        in_specs=[step_rows(width), whole(EDGE, width), whole(KW, width), step_rows(gates.shape[1])],
        out_specs=[step_rows(heads * DV), step_rows(heads * DK), whole(heads, DK, DK + DV)],
        out_shape=[
            jax.ShapeDtypeStruct((length, heads * DV), jnp.float32),
            jax.ShapeDtypeStruct((length, heads * DK), jnp.float32),
            jax.ShapeDtypeStruct((heads, DK, DK + DV), jnp.bfloat16),
        ],
        scratch_shapes=[
            pltpu.VMEM((CHUNK + EDGE, width), jnp.float32),
            pltpu.VMEM((CHUNK, width), jnp.bfloat16),
            pltpu.VMEM((heads, DK, DK + DV), jnp.float32),
        ],
        cost_estimate=pl.CostEstimate(flops=60 * 10**9, bytes_accessed=8 * 10**6, transcendentals=10**6),
        name="delta",
    )(joined, rim, taps, gates)


def finish_kernel(count, heads, core_ref, query_ref, z_ref, maps_ref, gain_ref, out_ref, state_ref):
    mine = lax.axis_index("ctx")

    @pl.when(pl.program_id(0) == 0)
    def _():
        state_ref[...] = jnp.zeros_like(state_ref)

        def hop(p, carry):
            @pl.when(p < mine)
            def _():
                for h in range(heads):
                    s = split(state_ref[h])
                    trans = maps_ref[p, h, :, :DK]
                    state_ref[h] = dot(trans, s[0]) + dot(trans, s[1]) + maps_ref[p, h, :, DK:].astype(jnp.float32)

            return carry

        lax.fori_loop(0, count - 1, hop, 0)

    for h in range(heads):
        span = slice(h * DV, (h + 1) * DV)
        core = core_ref[:, span] + MAIN(split(query_ref[:, span]), split(state_ref[h]))
        z = z_ref[:, span].astype(jnp.float32)
        mean = jnp.mean(core * core, -1, keepdims=True)
        out_ref[:, span] = (core * lax.rsqrt(mean + 1e-06) * gain_ref[...] * jax.nn.silu(z)).astype(jnp.bfloat16)


def finish(core, query, joined, maps, gain):
    length, wide = core.shape
    count, heads = maps.shape[:2]
    tile = min(256, length)
    step_rows = pl.BlockSpec((tile, wide), lambda i: (i, 0))
    return pl.pallas_call(
        functools.partial(finish_kernel, count, heads),
        grid=(length // tile,),
        in_specs=[step_rows, step_rows, pl.BlockSpec((tile, wide), lambda i: (i, joined.shape[1] // wide - 1)), pl.BlockSpec(maps.shape, lambda i: (0, 0, 0, 0)), pl.BlockSpec((1, DV), lambda i: (0, 0))],
        out_specs=step_rows,
        out_shape=jax.ShapeDtypeStruct((length, wide), jnp.bfloat16),
        scratch_shapes=[pltpu.VMEM((heads, DK, DV), jnp.float32)],
        cost_estimate=pl.CostEstimate(flops=10**9, bytes_accessed=8 * 10**6, transcendentals=10**6),
        name="finish",
    )(core, query, joined, maps, gain)


def ring_device(position, n):
    odd = lax.div(position, n // 2)
    return (1 - odd) * (2 * position) + odd * (2 * (n - 1 - position) + 1)


def gather_kernel(n, heads, act_ref, w_ref, act_out, w_out, act_tmp, w_tmp, local_sem, act_send, act_recv, ring_send, ring_recv):
    ctx, head = lax.axis_index("ctx"), lax.axis_index("head")
    odd = lax.rem(ctx, 2)
    position = (1 - odd) * lax.div(ctx, 2) + odd * (n - 1 - lax.div(ctx, 2))
    after = ring_device(lax.rem(position + 1, n), n)
    before = ring_device(lax.rem(position + n - 1, n), n)
    peers = [lax.rem(head + d, heads) for d in range(1, heads)]

    barrier = pltpu.get_barrier_semaphore()
    for other in (after, before):
        pl.semaphore_signal(barrier, inc=1, device_id=(other, head), device_id_type=pl.DeviceIdType.MESH)
    for peer in peers:
        pl.semaphore_signal(barrier, inc=1, device_id=(ctx, peer), device_id_type=pl.DeviceIdType.MESH)
    pl.semaphore_wait(barrier, heads + 1)

    piece = w_ref.shape[0] // (2 * SUBS)

    def hop(s, way, sub):
        offset = (way * SUBS + sub) * piece
        owner = ring_device(lax.rem(position + (n - s if way == 0 else s), n), n)
        place = w_out.at[owner, pl.ds(offset, piece)]
        return pltpu.make_async_remote_copy(
            src_ref=w_ref.at[pl.ds(offset, piece)] if s == 0 else place,
            dst_ref=place,
            send_sem=ring_send.at[s, way * SUBS + sub],
            recv_sem=ring_recv.at[s, way * SUBS + sub],
            device_id=(after if way == 0 else before, head),
            device_id_type=pl.DeviceIdType.MESH,
        )

    hops = [[hop(s, way, sub) for sub in range(SUBS) for way in range(2)] for s in range(n - 1)]
    for copy in hops[0]:
        copy.start()
    sends = [
        pltpu.make_async_remote_copy(
            src_ref=act_ref,
            dst_ref=act_out.at[head],
            send_sem=act_send.at[d],
            recv_sem=act_recv.at[d],
            device_id=(ctx, peer),
            device_id_type=pl.DeviceIdType.MESH,
        )
        for d, peer in enumerate(peers)
    ]
    for copy in sends:
        copy.start()
    take = [pltpu.make_async_copy(act_ref, act_tmp, local_sem.at[0]), pltpu.make_async_copy(w_ref, w_tmp, local_sem.at[1])]
    keep = [
        pltpu.make_async_copy(act_tmp, act_out.at[head], local_sem.at[2]),
        pltpu.make_async_copy(w_tmp, w_out.at[ctx], local_sem.at[3]),
    ]
    for copy in take:
        copy.start()
    for one, two in zip(take, keep):
        one.wait()
        two.start()
    for s in range(1, n - 1):
        for arrived, copy in zip(hops[s - 1], hops[s]):
            arrived.wait_recv()
            copy.start()
    for copy in hops[n - 2]:
        copy.wait_recv()
    for copy in sends:
        copy.wait_recv()
    for two in keep:
        two.wait()
    for copy in sends:
        copy.wait_send()
    for row in hops:
        for copy in row:
            copy.wait_send()


def gather_inputs(activations, weights):
    n, heads = lax.axis_size("ctx"), lax.axis_size("head")
    anywhere = pl.BlockSpec(memory_space=pl.ANY)
    act, w = pl.pallas_call(
        functools.partial(gather_kernel, n, heads),
        in_specs=[anywhere, anywhere],
        out_specs=[anywhere, anywhere],
        out_shape=[
            jax.ShapeDtypeStruct((heads,) + activations.shape, activations.dtype),
            jax.ShapeDtypeStruct((n,) + weights.shape, weights.dtype),
        ],
        scratch_shapes=[
            pltpu.VMEM(activations.shape, activations.dtype),
            pltpu.VMEM(weights.shape, weights.dtype),
            pltpu.SemaphoreType.DMA((4,)),
            pltpu.SemaphoreType.DMA((heads - 1,)),
            pltpu.SemaphoreType.DMA((heads - 1,)),
            pltpu.SemaphoreType.DMA((n - 1, 2 * SUBS)),
            pltpu.SemaphoreType.DMA((n - 1, 2 * SUBS)),
        ],
        compiler_params=pltpu.CompilerParams(collective_id=0, has_side_effects=True),
        name="gather_inputs",
    )(activations, weights)
    return act.reshape(-1, act.shape[-1]), w.reshape(-1, w.shape[-1])


def exchange_kernel(n, w_ref, w_out, w_tmp, local_sem, ring_send, ring_recv):
    ctx, head = lax.axis_index("ctx"), lax.axis_index("head")
    odd = lax.rem(ctx, 2)
    position = (1 - odd) * lax.div(ctx, 2) + odd * (n - 1 - lax.div(ctx, 2))
    after = ring_device(lax.rem(position + 1, n), n)
    before = ring_device(lax.rem(position + n - 1, n), n)

    barrier = pltpu.get_barrier_semaphore()
    for other in (after, before):
        pl.semaphore_signal(barrier, inc=1, device_id=(other, head), device_id_type=pl.DeviceIdType.MESH)
    pl.semaphore_wait(barrier, 2)

    piece = w_ref.shape[0] // (2 * SUBS)

    def hop(s, way, sub):
        offset = (way * SUBS + sub) * piece
        owner = ring_device(lax.rem(position + (n - s if way == 0 else s), n), n)
        place = w_out.at[owner, pl.ds(offset, piece)]
        return pltpu.make_async_remote_copy(
            src_ref=w_ref.at[pl.ds(offset, piece)] if s == 0 else place,
            dst_ref=place,
            send_sem=ring_send.at[s, way * SUBS + sub],
            recv_sem=ring_recv.at[s, way * SUBS + sub],
            device_id=(after if way == 0 else before, head),
            device_id_type=pl.DeviceIdType.MESH,
        )

    hops = [[hop(s, way, sub) for sub in range(SUBS) for way in range(2)] for s in range(n - 1)]
    for copy in hops[0]:
        copy.start()
    take = pltpu.make_async_copy(w_ref, w_tmp, local_sem.at[0])
    keep = pltpu.make_async_copy(w_tmp, w_out.at[ctx], local_sem.at[1])
    take.start()
    take.wait()
    keep.start()
    for s in range(1, n - 1):
        for arrived, copy in zip(hops[s - 1], hops[s]):
            arrived.wait_recv()
            copy.start()
    for copy in hops[n - 2]:
        copy.wait_recv()
    keep.wait()
    for row in hops:
        for copy in row:
            copy.wait_send()


def exchange(state):
    n = lax.axis_size("ctx")
    flat = state.reshape(-1, state.shape[-1])
    anywhere = pl.BlockSpec(memory_space=pl.ANY)
    maps = pl.pallas_call(
        functools.partial(exchange_kernel, n),
        in_specs=[anywhere],
        out_specs=anywhere,
        out_shape=jax.ShapeDtypeStruct((n,) + flat.shape, flat.dtype),
        scratch_shapes=[
            pltpu.VMEM(flat.shape, flat.dtype),
            pltpu.SemaphoreType.DMA((2,)),
            pltpu.SemaphoreType.DMA((n - 1, 2 * SUBS)),
            pltpu.SemaphoreType.DMA((n - 1, 2 * SUBS)),
        ],
        compiler_params=pltpu.CompilerParams(collective_id=1, has_side_effects=True),
        name="exchange",
    )(flat)
    return maps.reshape((n,) + state.shape)


def shards(activations, w_query, w_key, w_value, w_zgate, conv_query, conv_key, conv_value, gate_code, beta_code, norm_gain, w_out):
    count = lax.axis_size("ctx")
    gathered, weight = gather_inputs(activations, jnp.concatenate([w_query, w_key, w_value, w_zgate], 1))
    w_out, gathered = lax.optimization_barrier((w_out, gathered))
    out_weight = lax.all_gather(w_out, "ctx", axis=1, tiled=True)
    length = gathered.shape[0]
    conv_width = conv_query.shape[1] + conv_key.shape[1] + conv_value.shape[1]
    project = lambda x, w: jnp.dot(x, w, preferred_element_type=jnp.float32).astype(jnp.bfloat16)
    edge = lax.ppermute(gathered[length - EDGE :], "ctx", [(i, i + 1) for i in range(count - 1)])
    rim = project(edge, weight[:, :conv_width])
    joined = project(gathered, weight)
    heads = gate_code.shape[1]
    gates = jnp.concatenate(
        [
            -gate_code.astype(jnp.float32) / 1048576.0,
            beta_code.astype(jnp.float32) / 65536.0,
            jnp.zeros((length, 128 - 2 * heads), jnp.float32),
        ],
        1,
    )
    taps = jnp.concatenate([conv_query, conv_key, conv_value], 1)
    core, query, state = delta(joined, rim, taps, gates, conv_query.shape[1], heads)
    state, out_weight = lax.optimization_barrier((state, out_weight))
    maps = exchange(state)
    normed = finish(core, query, joined, maps, norm_gain.reshape(1, DV))
    mixed = jnp.dot(normed, out_weight, preferred_element_type=jnp.float32).astype(jnp.bfloat16)
    return lax.psum_scatter(mixed, "head", scatter_dimension=0, tiled=True)


def solution(mesh):
    return jax.shard_map(
        shards,
        mesh=mesh,
        in_specs=(
            P(("ctx", "head"), None),
            P("ctx", "head"),
            P("ctx", "head"),
            P("ctx", "head"),
            P("ctx", "head"),
            P(None, "head"),
            P(None, "head"),
            P(None, "head"),
            P("ctx", "head"),
            P("ctx", "head"),
            P(),
            P("head", "ctx"),
        ),
        out_specs=P(("ctx", "head"), None),
        check_vma=False,
    )
```
